128 devices in a mesh: req: 16 (over x, z), head: 8 (over y, core).
Axes of the slice: x: 4, y: 4, z: 4, core: 2. Of those that a mesh axis runs over, the one named last changes fastest.
Arguments:
- hidden: bfloat16 [512, 2048], P('req', 'head'), may hold values from -6 to 6
- lengths: int32 [512], P('req'), may hold values from 1 to 384, as said below
- expert_ids: int32 [512, 8], P('req'), may hold values from 0 to 63, all different within a row
- route_weights: float32 [512, 8], P('req'), may hold values from 0.25 to 2.5
- w_qkv: bfloat16 [3, 2048, 2048], P(None, None, 'head'), may hold values from -0.125 to 0.125
- w_out: bfloat16 [2048, 2048], P('head'), may hold values from -0.125 to 0.125
- k_cache: bfloat16 [512, 384, 16, 128], P('req', None, 'head'), may hold values from -400 to 400
- v_cache: bfloat16 [512, 384, 16, 128], P('req', None, 'head'), may hold values from -12 to 12
- w_in: bfloat16 [2048, 64, 2048], P(None, 'head', 'req'), may hold values from -0.125 to 0.125
- w_down: bfloat16 [64, 1024, 2048], P('head', 'req'), may hold values from -0.1875 to 0.1875
Outputs:
- output: bfloat16 [512, 2048], P('req', 'head')
The draws below stay inside these ranges and needn't reach their ends.
Inputs may be any that keep to these rules, and one draw needn't show every extreme that they name: `lengths`: some request has exactly 384 cached positions.
All inputs are finite; a program needn't handle non-finite values.
Results may differ from the reference program's by a relative error of at most 0.023.
Values may be sent and summed in bfloat16 or wider, within the bound.
A program may use at most 128 MiB of HBM per device.

```python
import math
import jax
import jax.numpy as jnp
from jax import lax

D = 2048
HEADS = 16
HEAD_DIM = 128
EXPERTS = 64
FF = 1024
TOPK = 8
UNIT_BLOCK = 64
MAX_LEN = 384
REQUESTS = 512


def draw_lengths(key, part):
    group_count = REQUESTS // 8 + 1
    levels = jax.random.randint(jax.random.fold_in(key, 11), (group_count,), 0, 4)
    ceiling = jnp.right_shift(jnp.full((group_count,), MAX_LEN, jnp.int32), levels.astype(jnp.int32))
    per_request = ceiling[jnp.arange(REQUESTS, dtype=jnp.int32) // 8]
    drawn = jax.random.randint(jax.random.fold_in(key, 12), (REQUESTS,), 1, per_request + 1)
    chosen = jax.random.randint(jax.random.fold_in(key, 13), (), 0, REQUESTS)
    return jnp.where(jnp.arange(REQUESTS, dtype=jnp.int32) == chosen, MAX_LEN, drawn).astype(jnp.int32)


def draw_k_cache(key, part):
    shape = (REQUESTS, MAX_LEN, HEADS, HEAD_DIM)
    values = jnp.clip(jax.random.normal(jax.random.fold_in(key, 21), shape, jnp.float32), -6.0, 6.0)
    return values.astype(jnp.bfloat16)


def draw_v_cache(key, part):
    shape = (REQUESTS, MAX_LEN, HEADS, HEAD_DIM)
    base = jnp.clip(jax.random.normal(jax.random.fold_in(key, 31), (REQUESTS, 1, HEADS, HEAD_DIM), jnp.float32), -6.0, 6.0)
    noise = jnp.clip(jax.random.normal(jax.random.fold_in(key, 32), shape, jnp.float32), -6.0, 6.0)
    return (base + noise).astype(jnp.bfloat16)


def block_levels(own_key, extent, cuts, smallest, top_value):
    def one(axis_at, shards_of):
        draws = jax.random.uniform(jax.random.fold_in(jax.random.fold_in(own_key, 6), axis_at), (shards_of,), jnp.float32, smallest / len(cuts), top_value / len(cuts))
        return jnp.repeat(jnp.exp(draws), extent[axis_at] // shards_of).reshape((-1,) + (1,) * (len(extent) - axis_at - 1))

    level = one(*cuts[0])
    for cut in cuts[1:]:
        level = level * one(*cut)
    return level


def different_ones(stream_key, rows, count, top, lift):
    ranking = jax.random.permutation(jax.random.fold_in(stream_key, 1), count)
    boost = ranking
    for power in range(3):
        boost = boost * boost // count
    boost = boost * lift // count
    chance = jax.random.randint(jax.random.fold_in(stream_key, 2), (rows, count), 0, 4096) + boost
    sure = jax.random.permutation(jax.random.fold_in(stream_key, 3), rows)[jnp.arange(count) % rows]
    chance = jnp.where(jnp.arange(rows)[:, None] == sure[None, :], 1 << 14, chance)
    priority = chance * count + jnp.arange(count)
    return lax.top_k(priority.astype(jnp.int32), top)[1].astype(jnp.int32)


def bell_draw(rng, extent, spread, reach, split=(), kind=jnp.bfloat16):
    level = block_levels(rng, extent, split, -0.22, 0.18) if split else 1.0
    array = jax.random.normal(rng, extent, jnp.float32) * spread * level
    return jnp.minimum(jnp.maximum(array, -reach), reach).astype(kind)


def setup_inputs(seed: int = 0) -> dict:
    splits = jax.random.split(jax.random.key(seed), 11)
    return {
        "hidden": bell_draw(splits[0], (REQUESTS, D), 1.0, 6.0, ((0, 16), (1, 8))),
        "lengths": draw_lengths(jax.random.fold_in(splits[10], 71), 0),
        "expert_ids": different_ones(splits[2], REQUESTS, EXPERTS, TOPK, 1024),
        "route_weights": jnp.clip(jnp.exp(math.log(2.5) - 2.3025851 * jax.random.uniform(splits[3], (REQUESTS, TOPK), jnp.float32) ** block_levels(splits[3], (REQUESTS, TOPK), ((0, 16),), -0.2, 0.2)), 0.25, 2.5),
        "w_qkv": bell_draw(splits[4], (3, D, HEADS * HEAD_DIM), D ** -0.5, 0.125, ((2, 8),)),
        "w_out": bell_draw(splits[5], (HEADS * HEAD_DIM, D), (HEADS * HEAD_DIM) ** -0.5, 0.125, ((0, 8),)),
        "k_cache": draw_k_cache(jax.random.fold_in(splits[10], 71), 0),
        "v_cache": draw_v_cache(jax.random.fold_in(splits[10], 71), 0),
        "w_in": bell_draw(splits[8], (D, EXPERTS, 2 * FF), D ** -0.5, 0.125, ((1, 8), (2, 16))),
        "w_down": bell_draw(splits[9], (EXPERTS, FF, D), FF ** -0.5, 0.1875, ((0, 8), (1, 16))),
    }


rope_theta = 50000.0
norm_eps = 1e-05

def rotate(values, positions):
    half_dim = values.shape[-1] // 2
    freqs = rope_theta ** (-jnp.arange(half_dim, dtype=jnp.float32) / half_dim)
    angles = positions.astype(jnp.float32)[:, None] * freqs[None, :]
    cosine = jnp.cos(angles)[:, None, :]
    sine = jnp.sin(angles)[:, None, :]
    first_half = values[..., :half_dim]
    second_half = values[..., half_dim:]
    return jnp.concatenate([first_half * cosine - second_half * sine, second_half * cosine + first_half * sine], axis=-1)

def rms_normed(values):
    return (values * lax.rsqrt(lax.optimization_barrier(jnp.mean(values * values, axis=-1, keepdims=True)) + norm_eps)).astype(jnp.bfloat16)

def reference(hidden, lengths, expert_ids, route_weights, w_qkv, w_out, k_cache, v_cache, w_in, w_down):
    hidden_f = hidden.astype(jnp.float32)
    normed = rms_normed(hidden_f)
    projected = jnp.einsum('td,cdn->ctn', normed.astype(jnp.float32), w_qkv.astype(jnp.float32))
    projected = projected.reshape(3, REQUESTS, HEADS, HEAD_DIM)
    query = rotate(projected[0], lengths).astype(jnp.bfloat16)
    key_new = rotate(projected[1], lengths).astype(jnp.bfloat16)
    value_new = projected[2].astype(jnp.bfloat16)
    score_scale = HEAD_DIM ** (-0.5)

    def one_request(inputs):
        query_row, key_row, value_row, keys, values, length = inputs
        scores = jnp.einsum('hd,lhd->hl', query_row.astype(jnp.float32), keys.astype(jnp.float32)) * score_scale
        scores = jnp.where(jnp.arange(MAX_LEN, dtype=jnp.int32)[None, :] < length, scores, -jnp.inf)
        self_score = lax.optimization_barrier(jnp.sum(query_row.astype(jnp.float32) * key_row.astype(jnp.float32), axis=-1)) * score_scale
        row_top = jnp.maximum(lax.optimization_barrier(jnp.max(scores, axis=-1)), self_score)
        exponent = jnp.exp(scores - row_top[:, None])
        self_exp = jnp.exp(self_score - row_top)
        denominator = lax.optimization_barrier(jnp.sum(exponent, axis=-1)) + self_exp
        weights = (exponent / denominator[:, None]).astype(jnp.bfloat16)
        self_weight = (self_exp / denominator).astype(jnp.bfloat16)
        summed = jnp.einsum('hl,lhd->hd', weights.astype(jnp.float32), values.astype(jnp.float32))
        summed = summed + self_weight.astype(jnp.float32)[:, None] * value_row.astype(jnp.float32)
        return summed.astype(jnp.bfloat16)
    attended = lax.map(one_request, (query, key_new, value_new, k_cache, v_cache, lengths))
    attended = attended.reshape(REQUESTS, HEADS * HEAD_DIM)
    resid = hidden_f + jnp.dot(attended, w_out, preferred_element_type=jnp.float32)
    mixed = rms_normed(resid)
    expert_range = jnp.arange(EXPERTS, dtype=jnp.int32)
    share = lax.optimization_barrier(jnp.sum(route_weights[:, :, None] * (expert_ids[:, :, None] == expert_range[None, None, :]).astype(jnp.float32), axis=1))

    def one_expert(accum, inputs):
        weight_in, weight_down, expert_share = inputs
        gate_up = jnp.dot(mixed, weight_in, preferred_element_type=jnp.float32)
        gate_up = gate_up.reshape(REQUESTS, FF // UNIT_BLOCK, 2, UNIT_BLOCK)
        gate = gate_up[:, :, 0, :].reshape(REQUESTS, FF)
        upward = gate_up[:, :, 1, :].reshape(REQUESTS, FF)
        units = (expert_share[:, None] * (jax.nn.silu(gate) * upward)).astype(jnp.bfloat16)
        return (accum + jnp.dot(units, weight_down, preferred_element_type=jnp.float32), None)
    moe_sum, unused = lax.scan(one_expert, jnp.zeros((REQUESTS, D), jnp.float32), (jnp.moveaxis(w_in, 1, 0), w_down, share.T))
    return (resid + moe_sum).astype(jnp.bfloat16)
```

```python
import functools

import jax
import jax.numpy as jnp
import numpy as np
from jax import lax
from jax.experimental import pallas as pl
from jax.experimental.pallas import tpu as pltpu
from jax.sharding import PartitionSpec as P

MESH = pl.DeviceIdType.MESH
BF = jnp.bfloat16
F32 = jnp.float32

D = 2048
ROWS = 32
TOKENS = 512
HD = 128
LEN = 384
COLS = 2 * LEN
rope_theta = 50000.0
norm_eps = 1e-05
SCALE = HD ** (-0.5)


def dot(a, b):
    return jnp.dot(a, b, preferred_element_type=F32)


def kernel(
    hidden_ref, len_ref, cos_ref, sin_ref, share_ref,
    wqkv_hbm, wout_hbm, k_hbm, v_hbm, win_hbm, wdown_hbm,
    out_ref,
    wqkv, wout, kbuf, vbuf, wraw, wrel, wdown,
    hid, qs, sc, att, cts, ctr, resid, gath, tshare, acc, ssq, units,
    psend, xrecv, ssum, ea_r, ea_f, eb_r, eb_f, a1, b1, ea2_r, ea2_f, eb2_r, eb2_f, csum, yrecv,
    ld_sem, hs_sem, hr_sem, cs_sem, cr_sem, ds_sem, dr_sem, ag_s, ag_r, dd_s, dd_r,
    ps_s, ps_r, rs_s, rs_r, ys_s, ys_r,
):
    me_r = lax.axis_index("req")
    me_h = lax.axis_index("head")
    x, z = me_r // 4, me_r % 4
    y, c = me_h // 2, me_h % 2
    xp, xm, x2 = (x + 1) % 4, (x + 3) % 4, (x + 2) % 4
    zp, zm, z2 = (z + 1) % 4, (z + 3) % 4, (z + 2) % 4
    dev_xp, dev_xm = (xp * 4 + z, me_h), (xm * 4 + z, me_h)
    dev_zp, dev_zm = (x * 4 + zp, me_h), (x * 4 + zm, me_h)
    other = (me_r, y * 2 + (1 - c))

    loads = []

    def load(src, dst):
        copy = pltpu.make_async_copy(src, dst, ld_sem.at[len(loads)])
        copy.start()
        loads.append(copy)
        return copy

    ld_wqkv = load(wqkv_hbm, wqkv)
    ld_win = load(win_hbm, wraw)
    ld_k = [load(k_hbm.at[pl.ds(8 * g, 8)], kbuf.at[pl.ds(8 * g, 8)]) for g in range(4)]
    ld_v = [load(v_hbm.at[pl.ds(8 * g, 8)], vbuf.at[pl.ds(8 * g, 8)]) for g in range(4)]
    ld_wout = [load(wout_hbm.at[:, pl.ds(256 * j, 256)], wout.at[j]) for j in range(8)]
    ld_wdown = [load(wdown_hbm.at[:, pl.ds(256 * j, 256)], wdown.at[j]) for j in range(8)]

    barrier = pltpu.get_barrier_semaphore()
    for k in range(1, 8):
        pl.semaphore_signal(
            barrier, inc=1, device_id=(me_r, (me_h + k) % 8), device_id_type=MESH
        )
    for dev in (dev_xp, dev_xm, dev_zp, dev_zm):
        pl.semaphore_signal(barrier, inc=1, device_id=dev, device_id_type=MESH)
    pl.semaphore_wait(barrier, 11)

    sends = []

    def push(src, dst, s_sem, r_sem, dev):
        copy = pltpu.make_async_remote_copy(
            src_ref=src, dst_ref=dst, send_sem=s_sem, recv_sem=r_sem,
            device_id=dev, device_id_type=MESH,
        )
        copy.start()
        sends.append(copy)
        return copy

    order = (4, 5, 3, 2, 6, 7, 1)
    got_hid = {
        k: push(
            hidden_ref, hid.at[me_h], hs_sem.at[k - 1], hr_sem.at[k - 1],
            (me_r, (me_h + k) % 8),
        )
        for k in order
    }

    class Ring:
        def __init__(self, idx, full, halves, me, plus, minus, dev_p, dev_m):
            self.idx, self.full, self.halves = idx, full, halves
            self.plus, self.minus, self.dev_p, self.dev_m, self.me = plus, minus, dev_p, dev_m, me

        def _push(self, ref, n, dev):
            return push(ref, ref, ag_s.at[self.idx, n], ag_r.at[self.idx, n], dev)

        def start(self):
            own = self.full(self.me)
            self.from_m = self._push(own, 0, self.dev_p)
            self.from_p = self._push(own, 1, self.dev_m)

        def relay_m(self):
            self.from_m.wait_recv()
            self.half0 = self._push(self.halves(self.minus)[0], 2, self.dev_p)

        def relay_p(self):
            self.from_p.wait_recv()
            self.half1 = self._push(self.halves(self.plus)[1], 3, self.dev_m)

        def finish0(self):
            self.half0.wait_recv()

        def finish1(self):
            self.half1.wait_recv()

    def along_x(idx, full, halves):
        return Ring(idx, full, halves, x, xp, xm, dev_xp, dev_xm)

    def along_z(idx, full, halves):
        return Ring(idx, full, halves, z, zp, zm, dev_zp, dev_zm)

    t1 = along_z(
        0,
        lambda a: tshare.at[x, a],
        lambda a: (tshare.at[x, a, pl.ds(0, 16)], tshare.at[x, a, pl.ds(16, 16)]),
    )
    t2 = along_x(
        1,
        lambda a: tshare.at[a],
        lambda a: (tshare.at[a, pl.ds(0, 2)], tshare.at[a, pl.ds(2, 2)]),
    )
    ring_a1 = along_z(
        2,
        lambda a: gath.at[pl.ds(0, 2), c, x, a],
        lambda a: (gath.at[0, c, x, a], gath.at[1, c, x, a]),
    )
    ring_b1 = along_x(
        3,
        lambda a: gath.at[pl.ds(2, 2), c, a, z],
        lambda a: (gath.at[2, c, a, z], gath.at[3, c, a, z]),
    )
    ring_a2 = along_x(
        4,
        lambda a: gath.at[pl.ds(0, 2), c, a],
        lambda a: (gath.at[0, c, a], gath.at[1, c, a]),
    )
    ring_b2 = along_z(
        5,
        lambda a: gath.at[pl.ds(2, 2), c, :, a],
        lambda a: (gath.at[2, c, :, a], gath.at[3, c, :, a]),
    )

    tshare[x, z] = share_ref[...]
    t1.start()

    ld_win.wait()
    row_i = lax.broadcasted_iota(jnp.int32, (256, 256), 0)
    col_i = lax.broadcasted_iota(jnp.int32, (256, 256), 1)
    perm = jnp.where(
        ((row_i & 31) == (col_i >> 3)) & ((row_i >> 5) == (col_i & 7)), 1.0, 0.0
    ).astype(BF)

    def relay_out(lo, hi):
        def body(it, carry):
            base = pl.multiple_of(it * 512, 512)
            out_base = pl.multiple_of(it * 64, 64)
            rhs = jnp.concatenate(
                [wraw[pl.ds(base, 256), :], wraw[pl.ds(base + 256, 256), :]], axis=1
            )
            res = dot(perm, rhs).astype(BF)
            for e in range(8):
                for s in range(2):
                    wrel[pl.ds(out_base + 32 * s, 32), 128 * e : 128 * (e + 1)] = res[
                        32 * e : 32 * (e + 1), 128 * s : 128 * (s + 1)
                    ]
            return carry

        lax.fori_loop(lo, hi, body, 0)

    relay_out(0, 16)

    ld_wqkv.wait()

    def project(block, slot):
        xf = block.astype(F32)
        return [dot(block, wqkv[i, slot]) for i in range(3)], jnp.sum(
            xf * xf, axis=-1, keepdims=True
        )

    proj, squares = project(hidden_ref[...], me_h)
    for k in (1, 7, 6, 2, 3, 5, 4):
        got_hid[k].wait_recv()
        slot = (me_h + 8 - k) % 8
        more, sq = project(hid[slot], slot)
        proj = [a + b for a, b in zip(proj, more)]
        squares = squares + sq
    rs = lax.rsqrt(squares * (1.0 / D) + norm_eps)
    cosine, sine = cos_ref[...], sin_ref[...]
    q_f, k_f, v_f = [], [], []
    for h in range(2):
        part = [p[:, HD * h : HD * (h + 1)] * rs for p in proj]

        def turned(v):
            swapped = jnp.concatenate([v[:, HD // 2 :], v[:, : HD // 2]], axis=1)
            return (v * cosine + swapped * sine).astype(BF).astype(F32)

        q_f.append(turned(part[0]))
        k_f.append(turned(part[1]))
        v_f.append(part[2].astype(BF).astype(F32))
        qs[h] = q_f[h]

    t1.relay_m()
    t1.relay_p()

    for copy in ld_k:
        copy.wait()
    owner16 = lax.broadcasted_iota(jnp.int32, (16, COLS), 0) & 7
    owner16s = lax.broadcasted_iota(jnp.int32, (16, HD), 0) & 7

    def score_group(g, carry):
        base = pl.multiple_of(g * 8, 8)
        query = qs[:, pl.ds(base, 8), :].reshape(16, HD).astype(BF)
        out = None
        for i in range(8):
            s = lax.dot_general(
                query, kbuf[g * 8 + i], (((1,), (1,)), ((), ())), preferred_element_type=F32
            )
            out = s if i == 0 else jnp.where(owner16 == i, s, out)
        sc[:, pl.ds(base, 8), :] = out.reshape(2, 8, COLS)
        return carry

    lax.fori_loop(0, 4, score_group, 0)

    t1.finish0()
    t1.finish1()
    t2.start()

    position = lax.broadcasted_iota(jnp.int32, (ROWS, COLS), 1)
    limit = len_ref[...] * 2
    self_w = []
    for h in range(2):
        valid = ((position & 1) == h) & (position < limit)
        s = jnp.where(valid, sc[h] * SCALE, -jnp.inf)
        self_score = jnp.sum(q_f[h] * k_f[h], axis=-1, keepdims=True) * SCALE
        top = jnp.maximum(jnp.max(s, axis=-1, keepdims=True), self_score)
        e = jnp.exp(s - top)
        self_e = jnp.exp(self_score - top)
        inv = 1.0 / (jnp.sum(e, axis=-1, keepdims=True) + self_e)
        sc[h] = e * inv
        self_w.append((self_e * inv).astype(BF).astype(F32))

    for copy in ld_v:
        copy.wait()

    def value_group(g, carry):
        base = pl.multiple_of(g * 8, 8)
        weights = sc[:, pl.ds(base, 8), :].reshape(16, COLS).astype(BF)
        out = None
        for i in range(8):
            s = dot(weights, vbuf[g * 8 + i])
            out = s if i == 0 else jnp.where(owner16s == i, s, out)
        att[:, pl.ds(base, 8), :] = out.reshape(2, 8, HD)
        return carry

    lax.fori_loop(0, 4, value_group, 0)
    attended = jnp.concatenate(
        [(att[h] + self_w[h] * v_f[h]).astype(BF) for h in range(2)], axis=1
    )

    for copy in ld_wout:
        copy.wait()
    for j in range(8):
        cts[j] = dot(attended, wout[j]).astype(BF)
    got_c = {
        k: push(
            cts.at[(me_h + k) % 8], ctr.at[me_h], cs_sem.at[k - 1], cr_sem.at[k - 1],
            (me_r, (me_h + k) % 8),
        )
        for k in order
    }
    t2.relay_m()
    t2.relay_p()
    relay_out(16, 32)
    total = hidden_ref[...].astype(F32) + cts[me_h].astype(F32)
    for k in (1, 7, 6, 2, 3, 5, 4):
        got_c[k].wait_recv()
        total = total + ctr[(me_h + 8 - k) % 8].astype(F32)
    resid[...] = total
    gath[y, c, x, z] = total.astype(BF)

    got_d = [
        push(
            gath.at[y, c, x, z], gath.at[y, c, x, z], ds_sem.at[k - 1], dr_sem.at[k - 1],
            (me_r, ((y + k) % 4) * 2 + c),
        )
        for k in (2, 1, 3)
    ]
    for copy in got_d:
        copy.wait_recv()

    pieces = []

    def hand(ref):
        n = len(pieces)
        pieces.append(push(ref, ref, dd_s.at[n], dd_r.at[n], other))
        return pieces[-1]

    ring_a1.start()
    ring_b1.start()
    ring_a1.relay_m()
    ring_b1.relay_m()
    ring_a1.relay_p()
    ring_b1.relay_p()
    ring_a1.finish0()
    ring_a1.finish1()
    ring_a2.start()
    a_own = hand(gath.at[pl.ds(0, 2), c, x])
    ring_b1.finish0()
    ring_b1.finish1()
    ring_b2.start()
    b_own = hand(gath.at[pl.ds(2, 2), c, :, z])

    def squares_of(rows):
        f = rows.astype(F32)
        f = f * f
        out = f[:, :128]
        for i in range(1, 8):
            out = out + f[:, 128 * i : 128 * (i + 1)]
        return out

    def gate_up(rows, first, store):
        def body(n, carry):
            cols = pl.ds(pl.multiple_of(n * 256, 256), 256)
            store(cols, dot(rows, wrel[first : first + 1024, cols]))
            return carry

        lax.fori_loop(0, 4, body, 0)

    def part_a(xx):
        rows = jnp.concatenate(
            [gath[yy, cc, xx].reshape(128, 256) for yy in (0, 1) for cc in (0, 1)], axis=1
        )
        ssq[xx] = squares_of(rows).reshape(4, ROWS, 128)

        def store(cols, val):
            acc[xx, :, :, cols] = val.reshape(4, ROWS, 256)

        gate_up(rows, 0, store)

    def part_b(zz):
        rows = jnp.concatenate(
            [gath[yy, cc, :, zz].reshape(128, 256) for yy in (2, 3) for cc in (0, 1)], axis=1
        )
        ssq[:, zz] += squares_of(rows).reshape(4, ROWS, 128)

        def store(cols, val):
            acc[:, zz, :, cols] += val.reshape(4, ROWS, 256)

        gate_up(rows, 1024, store)

    a_own.wait_recv()
    part_a(x)
    ring_a2.relay_m()
    a_m = hand(gath.at[pl.ds(0, 2), c, xm])
    ring_b2.relay_m()
    b_m = hand(gath.at[pl.ds(2, 2), c, :, zm])
    ring_a2.relay_p()
    a_p = hand(gath.at[pl.ds(0, 2), c, xp])
    ring_b2.relay_p()
    b_p = hand(gath.at[pl.ds(2, 2), c, :, zp])
    a_m.wait_recv()
    part_a(xm)
    a_p.wait_recv()
    part_a(xp)
    ring_a2.finish0()
    a_20 = hand(gath.at[0, c, x2])
    ring_a2.finish1()
    a_21 = hand(gath.at[1, c, x2])
    ring_b2.finish0()
    b_20 = hand(gath.at[2, c, :, z2])
    ring_b2.finish1()
    b_21 = hand(gath.at[3, c, :, z2])
    t2.finish0()
    t2.finish1()
    a_20.wait_recv()
    a_21.wait_recv()
    part_a(x2)
    b_own.wait_recv()
    part_b(z)
    b_m.wait_recv()
    part_b(zm)
    b_p.wait_recv()
    part_b(zp)
    b_20.wait_recv()
    b_21.wait_recv()
    part_b(z2)

    e_row = lax.broadcasted_iota(jnp.int32, (128, HD), 0)
    e_lane = lax.broadcasted_iota(jnp.int32, (128, HD), 1)
    low = lax.broadcasted_iota(jnp.int32, (128, HD), 1) < 64

    def unit_rows(xx, carry):
        mean = jnp.sum(ssq[xx].reshape(128, 128), axis=-1, keepdims=True) * (1.0 / D)
        scale = lax.rsqrt(mean + norm_eps)
        shares = tshare[xx].reshape(128, 128)
        for p in range(4):
            pick = jnp.where(
                (e_row < 16) & ((e_row & 7) == 2 * p + (e_lane >> 6)), 1.0, 0.0
            ).astype(BF)
            share = dot(shares, pick)
            even = acc[xx, :, :, 256 * p : 256 * p + 128].reshape(128, 128) * scale
            odd = acc[xx, :, :, 256 * p + 128 : 256 * p + 256].reshape(128, 128) * scale
            gate = jnp.where(low, even, pltpu.roll(odd, 64, 1))
            upward = jnp.where(low, pltpu.roll(even, 64, 1), odd)
            silu = gate / (1.0 + jnp.exp(-gate))
            units[xx, :, :, 128 * p : 128 * (p + 1)] = (
                (share * (silu * upward)).astype(BF).reshape(4, ROWS, 128)
            )
        return carry

    lax.fori_loop(0, 4, unit_rows, 0)

    for copy in ld_wdown:
        copy.wait()
    got_x = []
    for yy in range(4):
        def give(xx, carry, yy=yy):
            val = dot(units[xx].reshape(128, 512), wdown[yy * 2 + (1 - c)])
            psend[yy, xx] = val.astype(BF).reshape(4, ROWS, 256)
            return carry

        lax.fori_loop(0, 4, give, 0)
        got_x.append(push(psend.at[yy], xrecv.at[yy], ps_s.at[yy], ps_r.at[yy], other))

    def keep_block(yy):
        got_x[yy].wait_recv()

        def body(xx, carry):
            val = dot(units[xx].reshape(128, 512), wdown[yy * 2 + c])
            val = val + xrecv[yy, xx].reshape(128, 256).astype(F32)
            ssum[yy, xx] = val.astype(BF).reshape(4, ROWS, 256)
            return carry

        lax.fori_loop(0, 4, body, 0)

    class Reduce:
        def __init__(self, idx, ref, blk, relay, final, me, plus, minus, opp, dev_p, dev_m):
            self.idx, self.ref, self.blk, self.relay, self.final = idx, ref, blk, relay, final
            self.me, self.plus, self.minus, self.opp = me, plus, minus, opp
            self.dev_p, self.dev_m = dev_p, dev_m

        def _push(self, src, dst, n, dev):
            return push(src, dst, rs_s.at[self.idx, n], rs_r.at[self.idx, n], dev)

        def start(self):
            at = lambda hf, a: self.ref.at[self.blk(hf, a)]
            self.r0 = self._push(at(0, self.opp), self.relay.at[0], 0, self.dev_p)
            self.r1 = self._push(at(1, self.opp), self.relay.at[1], 1, self.dev_m)
            self.p1 = self._push(at(1, self.plus), self.final.at[0, 1], 2, self.dev_p)
            self.m0 = self._push(at(0, self.minus), self.final.at[1, 0], 3, self.dev_m)

        def _add(self, hf, a, got):
            i = self.blk(hf, a)
            self.ref[i] = (self.ref[i].astype(F32) + got.astype(F32)).astype(BF)

        def relay0(self):
            self.r0.wait_recv()
            self._add(0, self.plus, self.relay[0])
            self.p0 = self._push(
                self.ref.at[self.blk(0, self.plus)], self.final.at[0, 0], 4, self.dev_p
            )

        def relay1(self):
            self.r1.wait_recv()
            self._add(1, self.minus, self.relay[1])
            self.m1 = self._push(
                self.ref.at[self.blk(1, self.minus)], self.final.at[1, 1], 5, self.dev_m
            )

        def wait(self):
            for copy in (self.p1, self.m0, self.p0, self.m1):
                copy.wait_recv()

        def own(self, hf):
            return (
                self.ref[self.blk(hf, self.me)].astype(F32)
                + self.final[0, hf].astype(F32)
                + self.final[1, hf].astype(F32)
            )

    def reduce_x(idx, ref, blk, relay, final):
        return Reduce(idx, ref, blk, relay, final, x, xp, xm, x2, dev_xp, dev_xm)

    def reduce_z(idx, ref, blk, relay, final):
        return Reduce(idx, ref, blk, relay, final, z, zp, zm, z2, dev_zp, dev_zm)

    all4 = slice(None)
    ea1 = reduce_x(0, ssum, lambda hf, a: (hf, a), ea_r, ea_f)
    eb1 = reduce_z(1, ssum, lambda hf, a: (2 + hf, all4, a), eb_r, eb_f)
    ea2 = reduce_z(2, a1, lambda hf, a: (hf, a), ea2_r, ea2_f)
    eb2 = reduce_x(3, b1, lambda hf, a: (hf, a), eb2_r, eb2_f)

    keep_block(0)
    keep_block(1)
    ea1.start()
    keep_block(2)
    keep_block(3)
    eb1.start()
    ea1.relay0()
    ea1.relay1()
    eb1.relay0()
    eb1.relay1()
    ea1.wait()
    for hf in range(2):
        a1[hf] = ea1.own(hf).astype(BF)
    ea2.start()
    eb1.wait()
    for hf in range(2):
        b1[hf] = eb1.own(hf).astype(BF)
    eb2.start()
    ea2.relay0()
    ea2.relay1()
    eb2.relay0()
    eb2.relay1()
    ea2.wait()
    for hf in range(2):
        csum[hf] = ea2.own(hf).astype(BF)
    eb2.wait()
    for hf in range(2):
        csum[2 + hf] = eb2.own(hf).astype(BF)

    got_y = [
        push(
            csum.at[(y + k) % 4], yrecv.at[k - 1], ys_s.at[k - 1], ys_r.at[k - 1],
            (me_r, ((y + k) % 4) * 2 + c),
        )
        for k in (2, 1, 3)
    ]
    result = resid[...] + csum[y].astype(F32)
    for copy in got_y:
        copy.wait_recv()
    for k in range(3):
        result = result + yrecv[k].astype(F32)
    out_ref[...] = result.astype(BF)
    for copy in sends:
        copy.wait_send()


def layer(hidden, lengths, expert_ids, route_weights, w_qkv, w_out, k_cache, v_cache, w_in, w_down):
    half = HD // 2
    freqs = jnp.asarray(
        np.tile(rope_theta ** (-np.arange(half, dtype=np.float64) / half), 2).astype(np.float32)
    )
    sign = jnp.asarray(np.repeat([-1.0, 1.0], half).astype(np.float32))
    angles = lengths.astype(F32)[:, None] * freqs[None, :]
    cosine, sine = jnp.cos(angles), jnp.sin(angles) * sign[None, :]
    lane = jnp.arange(128, dtype=jnp.int32)
    wanted = lax.axis_index("head") * 8 + (lane & 7)
    share = jnp.sum(
        route_weights[:, :, None] * (expert_ids[:, :, None] == wanted[None, None, :]).astype(F32),
        axis=1,
    )
    high = share.astype(BF)
    lower = (share - high.astype(F32)).astype(BF)
    share = jnp.where(lane < 8, high, jnp.where(lane < 16, lower, jnp.zeros_like(high)))

    vm = pl.BlockSpec(memory_space=pltpu.VMEM)
    hbm = pl.BlockSpec(memory_space=pl.ANY)
    V = pltpu.VMEM
    dma = pltpu.SemaphoreType.DMA
    return pl.pallas_call(
        kernel,
        out_shape=jax.ShapeDtypeStruct((ROWS, 256), BF),
        in_specs=[vm] * 5 + [hbm] * 6,
        out_specs=vm,
        scratch_shapes=[
            V((3, 8, 256, 256), BF), V((8, 256, 256), BF), V((ROWS, COLS, HD), BF),
            V((ROWS, COLS, HD), BF), V((16384, 128), BF), V((2048, 1024), BF), V((8, 512, 256), BF),
            V((8, ROWS, 256), BF), V((2, ROWS, HD), F32), V((2, ROWS, COLS), F32),
            V((2, ROWS, HD), F32), V((8, ROWS, 256), BF), V((8, ROWS, 256), BF),
            V((ROWS, 256), F32), V((4, 2, 4, 4, ROWS, 256), BF), V((4, 4, ROWS, 128), BF),
            V((4, 4, ROWS, 1024), F32), V((4, 4, ROWS, 128), F32), V((4, 4, ROWS, 512), BF),
            V((4, 4, 4, ROWS, 256), BF), V((4, 4, 4, ROWS, 256), BF), V((4, 4, 4, ROWS, 256), BF),
            V((2, 4, ROWS, 256), BF), V((2, 2, 4, ROWS, 256), BF),
            V((2, 4, ROWS, 256), BF), V((2, 2, 4, ROWS, 256), BF),
            V((2, 4, ROWS, 256), BF), V((2, 4, ROWS, 256), BF),
            V((2, ROWS, 256), BF), V((2, 2, ROWS, 256), BF),
            V((2, ROWS, 256), BF), V((2, 2, ROWS, 256), BF),
            V((4, ROWS, 256), BF), V((3, ROWS, 256), BF),
            dma((26,)), dma((7,)), dma((7,)), dma((7,)), dma((7,)), dma((3,)), dma((3,)),
            dma((6, 4)), dma((6, 4)), dma((10,)), dma((10,)),
            dma((4,)), dma((4,)), dma((4, 6)), dma((4, 6)), dma((3,)), dma((3,)),
        ],
        compiler_params=pltpu.CompilerParams(
            collective_id=0, has_side_effects=True, vmem_limit_bytes=60 * 1024 * 1024
        ),
    )(
        hidden, lengths[:, None], cosine, sine, share,
        w_qkv.reshape(3, 8, 256, 256), w_out,
        k_cache.reshape(ROWS, COLS, HD), v_cache.reshape(ROWS, COLS, HD),
        w_in.reshape(16384, 128), w_down.reshape(512, D),
    )


def solution(mesh):
    in_specs = (
        P("req", "head"),
        P("req"),
        P("req", None),
        P("req", None),
        P(None, None, "head"),
        P("head", None),
        P("req", None, "head", None),
        P("req", None, "head", None),
        P(None, "head", "req"),
        P("head", "req", None),
    )
    return jax.shard_map(
        layer, mesh=mesh, in_specs=in_specs, out_specs=P("req", "head"), check_vma=False
    )
```

```python
import functools

import jax
import jax.numpy as jnp
import numpy as np
from jax import lax
from jax.experimental import pallas as pl
from jax.experimental.pallas import tpu as pltpu
from jax.sharding import PartitionSpec as P

MESH = pl.DeviceIdType.MESH
BF = jnp.bfloat16
F32 = jnp.float32

D = 2048
ROWS = 32
TOKENS = 512
HD = 128
LEN = 384
COLS = 2 * LEN
rope_theta = 50000.0
norm_eps = 1e-05
SCALE = HD ** (-0.5)


def dot(a, b):
    return jnp.dot(a, b, preferred_element_type=F32)


def kernel(
    freq_ref, sign_ref, hidden_ref, len_ref, ids_ref, rw_ref,
    wqkv_hbm, wout_hbm, k_hbm, v_hbm, win_hbm, wdown_hbm,
    out_ref,
    wqkv, wout, kbuf, vbuf, wraw, wrel, wdown,
    hid, qs, sc, att, cts, ctr, resid, gath, tshare, xs, units, psend, xrecv, ssum, yrecv,
    ld_sem, hs_sem, hr_sem, cs_sem, cr_sem, t_s, t_r, d_s, d_r, dd_s, dd_r,
    ps_s, ps_r, e_s, e_r, plane_sem, cube_sem,
):
    me_r = lax.axis_index("req")
    me_h = lax.axis_index("head")
    x, z = me_r // 4, me_r % 4
    y, c = me_h // 2, me_h % 2
    other = (me_r, y * 2 + (1 - c))

    def at(dx, dy, dz):
        return ((x + dx) % 4) * 4 + (z + dz) % 4, ((y + dy) % 4) * 2 + c

    loads = []

    def load(src, dst):
        copy = pltpu.make_async_copy(src, dst, ld_sem.at[len(loads)])
        copy.start()
        loads.append(copy)
        return copy

    ld_wqkv = load(wqkv_hbm, wqkv)
    ld_k = [load(k_hbm.at[pl.ds(8 * g, 8)], kbuf.at[pl.ds(8 * g, 8)]) for g in range(4)]
    ld_v = [load(v_hbm.at[pl.ds(8 * g, 8)], vbuf.at[pl.ds(8 * g, 8)]) for g in range(4)]
    ld_wout = [load(wout_hbm.at[:, pl.ds(256 * j, 256)], wout.at[j]) for j in range(8)]
    ld_win = load(win_hbm, wraw)
    ld_wdown = [load(wdown_hbm.at[:, pl.ds(256 * j, 256)], wdown.at[j]) for j in range(8)]

    barrier = pltpu.get_barrier_semaphore()

    def tell(sem, dev):
        pl.semaphore_signal(sem, inc=1, device_id=dev, device_id_type=MESH)

    for k in range(1, 8):
        tell(barrier, (me_r, (me_h + k) % 8))
    for k in range(1, 4):
        tell(barrier, at(k, 0, 0))
        tell(barrier, at(0, 0, k))

    expert = lax.broadcasted_iota(jnp.int32, (8, ROWS), 0) + me_h * 8
    share = jnp.zeros((8, ROWS), F32)
    for k in range(8):
        share = share + jnp.where(ids_ref[k : k + 1, :] == expert, rw_ref[k : k + 1, :], 0.0)
    high = share.astype(BF)
    lower = (share - high.astype(F32)).astype(BF)
    both = jnp.concatenate([high.astype(F32), lower.astype(F32)], axis=0).astype(BF)
    eye = jnp.where(
        lax.broadcasted_iota(jnp.int32, (16, 128), 0)
        == lax.broadcasted_iota(jnp.int32, (16, 128), 1),
        1.0,
        0.0,
    ).astype(BF)
    tshare[z, x] = lax.dot_general(
        both, eye, (((0,), (0,)), ((), ())), preferred_element_type=F32
    ).astype(BF)
    length = jnp.sum(
        jnp.where(
            lax.broadcasted_iota(jnp.int32, (ROWS, ROWS), 0)
            == lax.broadcasted_iota(jnp.int32, (ROWS, ROWS), 1),
            len_ref[...].astype(F32),
            0.0,
        ),
        axis=1,
        keepdims=True,
    )
    angles = length * freq_ref[...]
    cosine, sine = jnp.cos(angles), jnp.sin(angles) * sign_ref[...]
    limit = length.astype(jnp.int32) * 2

    pl.semaphore_wait(barrier, 13)

    def remote(src, dst, s_sem, r_sem, dev):
        return pltpu.make_async_remote_copy(
            src_ref=src, dst_ref=dst, send_sem=s_sem, recv_sem=r_sem,
            device_id=dev, device_id_type=MESH,
        )

    sends = []

    def push(src, dst, s_sem, r_sem, dev):
        copy = remote(src, dst, s_sem, r_sem, dev)
        copy.start()
        sends.append(copy)
        return copy

    order = (4, 5, 3, 2, 6, 7, 1)
    got_hid = {
        k: push(
            hidden_ref, hid.at[me_h], hs_sem.at[k - 1], hr_sem.at[k - 1],
            (me_r, (me_h + k) % 8),
        )
        for k in order
    }
    for k in range(1, 4):
        tell(plane_sem, at(0, 0, k))

    row_i = lax.broadcasted_iota(jnp.int32, (256, 256), 0)
    col_i = lax.broadcasted_iota(jnp.int32, (256, 256), 1)
    perm = jnp.where(
        ((row_i & 31) == (col_i >> 3)) & ((row_i >> 5) == (col_i & 7)), 1.0, 0.0
    ).astype(BF)

    def relay_out(lo, hi):
        def body(it, carry):
            base = pl.multiple_of(it * 512, 512)
            out_base = pl.multiple_of(it * 64, 64)
            rhs = jnp.concatenate(
                [wraw[pl.ds(base, 256), :], wraw[pl.ds(base + 256, 256), :]], axis=1
            )
            res = dot(perm, rhs).astype(BF)
            for e in range(8):
                for s in range(2):
                    wrel[pl.ds(out_base + 32 * s, 32), 128 * e : 128 * (e + 1)] = res[
                        32 * e : 32 * (e + 1), 128 * s : 128 * (s + 1)
                    ]
            return carry

        lax.fori_loop(lo, hi, body, 0)

    ld_wqkv.wait()

    def project(block, slot):
        xf = block.astype(F32)
        return [dot(block, wqkv[i, slot]) for i in range(3)], jnp.sum(
            xf * xf, axis=-1, keepdims=True
        )

    proj, squares = project(hidden_ref[...], me_h)
    for k in (1, 7, 6, 2, 3, 5, 4):
        got_hid[k].wait_recv()
        slot = (me_h + 8 - k) % 8
        more, sq = project(hid[slot], slot)
        proj = [a + b for a, b in zip(proj, more)]
        squares = squares + sq
    rs = lax.rsqrt(squares * (1.0 / D) + norm_eps)
    q_f, k_f, v_f = [], [], []
    for h in range(2):
        part = [p[:, HD * h : HD * (h + 1)] * rs for p in proj]

        def turned(v):
            swapped = jnp.concatenate([v[:, HD // 2 :], v[:, : HD // 2]], axis=1)
            return (v * cosine + swapped * sine).astype(BF).astype(F32)

        q_f.append(turned(part[0]))
        k_f.append(turned(part[1]))
        v_f.append(part[2].astype(BF).astype(F32))
        qs[h] = q_f[h]

    pl.semaphore_wait(plane_sem, 3)
    for k in range(1, 4):
        tell(cube_sem, at(0, k, 0))

    def send_share(i, carry):
        remote(tshare.at[z, x], tshare.at[z, x], t_s, t_r, at(i // 4, 0, i % 4)).start()
        return carry

    lax.fori_loop(1, 16, send_share, 0)

    for copy in ld_k:
        copy.wait()
    owner16 = lax.broadcasted_iota(jnp.int32, (16, COLS), 0) & 7
    owner16s = lax.broadcasted_iota(jnp.int32, (16, HD), 0) & 7

    def score_group(g, carry):
        base = pl.multiple_of(g * 8, 8)
        query = qs[:, pl.ds(base, 8), :].reshape(16, HD).astype(BF)
        out = None
        for i in range(8):
            s = lax.dot_general(
                query, kbuf[g * 8 + i], (((1,), (1,)), ((), ())), preferred_element_type=F32
            )
            out = s if i == 0 else jnp.where(owner16 == i, s, out)
        sc[:, pl.ds(base, 8), :] = out.reshape(2, 8, COLS)
        return carry

    lax.fori_loop(0, 4, score_group, 0)

    position = lax.broadcasted_iota(jnp.int32, (ROWS, COLS), 1)
    self_w = []
    for h in range(2):
        valid = ((position & 1) == h) & (position < limit)
        s = jnp.where(valid, sc[h] * SCALE, -jnp.inf)
        self_score = jnp.sum(q_f[h] * k_f[h], axis=-1, keepdims=True) * SCALE
        top = jnp.maximum(jnp.max(s, axis=-1, keepdims=True), self_score)
        e = jnp.exp(s - top)
        self_e = jnp.exp(self_score - top)
        inv = 1.0 / (jnp.sum(e, axis=-1, keepdims=True) + self_e)
        sc[h] = e * inv
        self_w.append((self_e * inv).astype(BF).astype(F32))

    for copy in ld_v:
        copy.wait()

    def value_group(g, carry):
        base = pl.multiple_of(g * 8, 8)
        weights = sc[:, pl.ds(base, 8), :].reshape(16, COLS).astype(BF)
        out = None
        for i in range(8):
            s = dot(weights, vbuf[g * 8 + i])
            out = s if i == 0 else jnp.where(owner16s == i, s, out)
        att[:, pl.ds(base, 8), :] = out.reshape(2, 8, HD)
        return carry

    lax.fori_loop(0, 4, value_group, 0)
    attended = jnp.concatenate(
        [(att[h] + self_w[h] * v_f[h]).astype(BF) for h in range(2)], axis=1
    )

    for copy in ld_wout:
        copy.wait()
    for j in range(8):
        cts[j] = dot(attended, wout[j]).astype(BF)
    got_c = {
        k: push(
            cts.at[(me_h + k) % 8], ctr.at[me_h], cs_sem.at[k - 1], cr_sem.at[k - 1],
            (me_r, (me_h + k) % 8),
        )
        for k in order
    }
    ld_win.wait()
    relay_out(0, 16)
    total = hidden_ref[...].astype(F32) + cts[me_h].astype(F32)
    for k in (1, 7, 6, 2, 3, 5, 4):
        got_c[k].wait_recv()
        total = total + ctr[(me_h + 8 - k) % 8].astype(F32)
    resid[...] = total
    gath[z, c, y, x] = total.astype(BF)

    pl.semaphore_wait(cube_sem, 3)
    for dz in (0, 1, 3, 2):
        def send_rows(i, carry, dz=dz):
            remote(
                gath.at[z, c, y, x], gath.at[z, c, y, x], d_s, d_r.at[(4 - dz) % 4],
                at(i // 4, i % 4, dz),
            ).start()
            return carry

        lax.fori_loop(1 if dz == 0 else 0, 16, send_rows, 0)

    relay_out(16, 32)
    remote(
        kbuf.at[pl.ds(0, 15), pl.ds(0, ROWS)], kbuf.at[pl.ds(0, 15), pl.ds(0, ROWS)],
        t_s, t_r, other,
    ).wait_recv()

    def collect(g):
        zz = (z + g) % 4
        whole = yrecv.at[pl.ds(0, 15 if g == 0 else 16)]
        remote(whole, whole, d_s, d_r.at[g], other).wait_recv()
        return push(gath.at[zz, c], gath.at[zz, c], dd_s.at[g], dd_r.at[g], other)

    e_row = lax.broadcasted_iota(jnp.int32, (128, HD), 0)
    e_lane = lax.broadcasted_iota(jnp.int32, (128, HD), 1)

    def gate_up(group):
        m = 128 * len(group)
        scales, shares = [], []
        for i, g in enumerate(group):
            zz = (z + g) % 4
            part = None
            for j in range(8):
                block = gath[zz, j % 2, j // 2].reshape(128, 256)
                xs[128 * i : 128 * (i + 1), 256 * j : 256 * (j + 1)] = block
                f = block.astype(F32)
                f = f * f
                f = f[:, :128] + f[:, 128:]
                part = f if part is None else part + f
            mean = jnp.sum(part, axis=-1, keepdims=True) * (1.0 / D)
            scales.append(lax.rsqrt(mean + norm_eps))
            shares.append(tshare[zz].reshape(128, 128))
        scale = jnp.concatenate(scales, axis=0)
        shares = jnp.concatenate(shares, axis=0)
        low = lax.broadcasted_iota(jnp.int32, (m, HD), 1) < 64

        def body(n, carry):
            cols = pl.ds(pl.multiple_of(n * 256, 256), 256)
            got = dot(xs[:m, :], wrel[:, cols])
            pick = jnp.where(
                (e_row < 16) & ((e_row & 7) == 2 * n + (e_lane >> 6)), 1.0, 0.0
            ).astype(BF)
            share = dot(shares, pick)
            even = got[:, :128] * scale
            odd = got[:, 128:] * scale
            gate = jnp.where(low, even, pltpu.roll(odd, 64, 1))
            upward = jnp.where(low, pltpu.roll(even, 64, 1), odd)
            silu = gate / (1.0 + jnp.exp(-gate))
            units[:m, pl.ds(pl.multiple_of(n * 128, 128), 128)] = (
                share * (silu * upward)
            ).astype(BF)
            return carry

        lax.fori_loop(0, 4, body, 0)

    turns = (2, 1, 3, 0)
    got_x = {}

    def give(group):
        m = 128 * len(group)
        for dy in turns:
            val = dot(units[:m, :], wdown[((y + dy) % 4) * 2 + (1 - c)]).astype(BF)
            for i, g in enumerate(group):
                psend[g, dy] = val[128 * i : 128 * (i + 1)].reshape(4, ROWS, 256)
                got_x[g, dy] = push(
                    psend.at[g, dy], xrecv.at[g, dy], ps_s.at[g, dy], ps_r.at[g, dy], other
                )

    def keep(group):
        m = 128 * len(group)
        for dy in turns:
            val = dot(units[:m, :], wdown[((y + dy) % 4) * 2 + c])
            for i, g in enumerate(group):
                got_x[g, dy].wait_recv()
                mine = val[128 * i : 128 * (i + 1)] + xrecv[g, dy].reshape(128, 256).astype(F32)
                ssum[g, dy] = mine.astype(BF).reshape(4, ROWS, 256)

                def send_sum(dx, carry, dy=dy, g=g):
                    xx = (x + dx) % 4
                    slot = ((4 - g) % 4) * 16 + ((4 - dx) % 4) * 4 + (4 - dy) % 4
                    remote(
                        ssum.at[g, dy, xx], yrecv.at[slot], e_s, e_r.at[(4 - g) % 4],
                        at(dx, dy, g),
                    ).start()
                    return carry

                lax.fori_loop(1 if g == 0 and dy == 0 else 0, 4, send_sum, 0)

    for copy in ld_wdown:
        copy.wait()
    first = collect(0)
    first.wait_recv()
    gate_up((0,))
    give((0,))
    near = [collect(1), collect(3)]
    keep((0,))
    for copy in near:
        copy.wait_recv()
    gate_up((1, 3))
    give((1, 3))
    last = collect(2)
    keep((1, 3))
    last.wait_recv()
    gate_up((2,))
    give((2,))
    keep((2,))

    result = resid[...] + ssum[0, 0, x].astype(F32)
    for g in (0, 1, 3, 2):
        first_slot = 16 * g + (1 if g == 0 else 0)
        slots = pl.ds(first_slot, 15 if g == 0 else 16)
        remote(yrecv.at[slots], yrecv.at[slots], e_s, e_r.at[g], other).wait_recv()
        for i in range(first_slot, 16 * g + 16):
            result = result + yrecv[i].astype(F32)
    out_ref[...] = result.astype(BF)
    for copy in sends:
        copy.wait_send()
    cells = yrecv.at[pl.ds(1, 63)]
    remote(cells, cells, d_s, d_r.at[0], other).wait_send()
    remote(cells, cells, e_s, e_r.at[0], other).wait_send()
    few = kbuf.at[pl.ds(0, 15), pl.ds(0, ROWS)]
    remote(few, few, t_s, t_r, other).wait_send()


def layer(hidden, lengths, expert_ids, route_weights, w_qkv, w_out, k_cache, v_cache, w_in, w_down):
    half = HD // 2
    freqs = np.tile(rope_theta ** (-np.arange(half, dtype=np.float64) / half), 2)
    sign = np.repeat([-1.0, 1.0], half)

    vm = pl.BlockSpec(memory_space=pltpu.VMEM)
    hbm = pl.BlockSpec(memory_space=pl.ANY)
    V = pltpu.VMEM
    dma = pltpu.SemaphoreType.DMA
    regular = pltpu.SemaphoreType.REGULAR
    return pl.pallas_call(
        kernel,
        out_shape=jax.ShapeDtypeStruct((ROWS, 256), BF),
        in_specs=[vm] * 6 + [hbm] * 6,
        out_specs=vm,
        scratch_shapes=[
            V((3, 8, 256, 256), BF), V((8, 256, 256), BF), V((ROWS, COLS, HD), BF),
            V((ROWS, COLS, HD), BF), V((16384, 128), BF), V((2048, 1024), BF), V((8, 512, 256), BF),
            V((8, ROWS, 256), BF), V((2, ROWS, HD), F32), V((2, ROWS, COLS), F32),
            V((2, ROWS, HD), F32), V((8, ROWS, 256), BF), V((8, ROWS, 256), BF),
            V((ROWS, 256), F32), V((4, 2, 4, 4, ROWS, 256), BF), V((4, 4, ROWS, 128), BF),
            V((256, D), BF), V((256, 512), BF),
            V((4, 4, 4, ROWS, 256), BF), V((4, 4, 4, ROWS, 256), BF), V((4, 4, 4, ROWS, 256), BF),
            V((64, ROWS, 256), BF),
            dma((26,)), dma((7,)), dma((7,)), dma((7,)), dma((7,)), dma, dma, dma, dma((4,)),
            dma((4,)), dma((4,)), dma((4, 4)), dma((4, 4)), dma, dma((4,)), regular, regular,
        ],
        compiler_params=pltpu.CompilerParams(
            collective_id=0, has_side_effects=True, vmem_limit_bytes=60 * 1024 * 1024
        ),
    )(
        jnp.asarray(freqs.astype(np.float32)[None, :]), jnp.asarray(sign.astype(np.float32)[None, :]),
        hidden, lengths[None, :], expert_ids.T, route_weights.T,
        w_qkv.reshape(3, 8, 256, 256), w_out,
        k_cache.reshape(ROWS, COLS, HD), v_cache.reshape(ROWS, COLS, HD),
        w_in.reshape(16384, 128), w_down.reshape(512, D),
    )


def solution(mesh):
    in_specs = (
        P("req", "head"),
        P("req"),
        P("req", None),
        P("req", None),
        P(None, None, "head"),
        P("head", None),
        P("req", None, "head", None),
        P("req", None, "head", None),
        P(None, "head", "req"),
        P("head", "req", None),
    )
    return jax.shard_map(
        layer, mesh=mesh, in_specs=in_specs, out_specs=P("req", "head"), check_vma=False
    )
```

```python
import functools

import jax
import jax.numpy as jnp
import numpy as np
from jax import lax
from jax.experimental import pallas as pl
from jax.experimental.pallas import tpu as pltpu
from jax.sharding import PartitionSpec as P

MESH = pl.DeviceIdType.MESH
BF = jnp.bfloat16
F32 = jnp.float32

D = 2048
ROWS = 32
TOKENS = 512
HD = 128
LEN = 384
COLS = 2 * LEN
rope_theta = 50000.0
norm_eps = 1e-05
SCALE = HD ** (-0.5)


def dot(a, b):
    return jnp.dot(a, b, preferred_element_type=F32)


def kernel(
    freq_ref, sign_ref, hidden_ref, len_ref, ids_ref, rw_ref,
    wqkv_hbm, wout_hbm, k_hbm, v_hbm, win_hbm, wdown_hbm,
    out_ref,
    wqkv, wout, kbuf, vbuf, wraw, wrel, wdown,
    hid, qs, sc, att, cts, ctr, resid, gath, tshare, xs, units, psend, xrecv, ssum, yrecv,
    ld_sem, hs_sem, hr_sem, cs_sem, cr_sem, t_s, t_r, d_s, d_r, dd_s, dd_r,
    ps_s, ps_r, e_s, e_r, plane_sem, cube_sem,
):
    me_r = lax.axis_index("req")
    me_h = lax.axis_index("head")
    x, z = me_r // 4, me_r % 4
    y, c = me_h // 2, me_h % 2
    other = (me_r, y * 2 + (1 - c))

    def at(dx, dy, dz):
        return ((x + dx) % 4) * 4 + (z + dz) % 4, ((y + dy) % 4) * 2 + c

    loads = []

    def load(src, dst):
        copy = pltpu.make_async_copy(src, dst, ld_sem.at[len(loads)])
        copy.start()
        loads.append(copy)
        return copy

    ld_wqkv = load(wqkv_hbm, wqkv)
    ld_k = [load(k_hbm.at[pl.ds(8 * g, 8)], kbuf.at[pl.ds(8 * g, 8)]) for g in range(4)]
    ld_v = [load(v_hbm.at[pl.ds(8 * g, 8)], vbuf.at[pl.ds(8 * g, 8)]) for g in range(4)]
    ld_wout = [load(wout_hbm.at[:, pl.ds(256 * j, 256)], wout.at[j]) for j in range(8)]
    ld_win = load(win_hbm, wraw)
    ld_wdown = [load(wdown_hbm.at[:, pl.ds(256 * j, 256)], wdown.at[j]) for j in range(8)]

    barrier = pltpu.get_barrier_semaphore()

    def tell(sem, dev):
        pl.semaphore_signal(sem, inc=1, device_id=dev, device_id_type=MESH)

    for k in range(1, 8):
        tell(barrier, (me_r, (me_h + k) % 8))
    for k in range(1, 4):
        tell(barrier, at(k, 0, 0))
        tell(barrier, at(0, 0, k))

    expert = lax.broadcasted_iota(jnp.int32, (8, ROWS), 0) + me_h * 8
    share = jnp.zeros((8, ROWS), F32)
    for k in range(8):
        share = share + jnp.where(ids_ref[k : k + 1, :] == expert, rw_ref[k : k + 1, :], 0.0)
    high = share.astype(BF)
    lower = (share - high.astype(F32)).astype(BF)
    both = jnp.concatenate([high.astype(F32), lower.astype(F32)], axis=0).astype(BF)
    eye = jnp.where(
        lax.broadcasted_iota(jnp.int32, (16, 128), 0)
        == lax.broadcasted_iota(jnp.int32, (16, 128), 1),
        1.0,
        0.0,
    ).astype(BF)
    tshare[z, x] = lax.dot_general(
        both, eye, (((0,), (0,)), ((), ())), preferred_element_type=F32
    ).astype(BF)
    length = jnp.sum(
        jnp.where(
            lax.broadcasted_iota(jnp.int32, (ROWS, ROWS), 0)
            == lax.broadcasted_iota(jnp.int32, (ROWS, ROWS), 1),
            len_ref[...].astype(F32),
            0.0,
        ),
        axis=1,
        keepdims=True,
    )
    angles = length * freq_ref[...]
    cosine, sine = jnp.cos(angles), jnp.sin(angles) * sign_ref[...]
    limit = length.astype(jnp.int32) * 2

    pl.semaphore_wait(barrier, 13)

    def remote(src, dst, s_sem, r_sem, dev):
        return pltpu.make_async_remote_copy(
            src_ref=src, dst_ref=dst, send_sem=s_sem, recv_sem=r_sem,
            device_id=dev, device_id_type=MESH,
        )

    sends = []

    def push(src, dst, s_sem, r_sem, dev):
        copy = remote(src, dst, s_sem, r_sem, dev)
        copy.start()
        sends.append(copy)
        return copy

    order = (4, 5, 3, 2, 6, 7, 1)
    got_hid = {
        k: push(
            hidden_ref, hid.at[me_h], hs_sem.at[k - 1], hr_sem.at[k - 1],
            (me_r, (me_h + k) % 8),
        )
        for k in order
    }
    for k in range(1, 4):
        tell(plane_sem, at(0, 0, k))

    row_i = lax.broadcasted_iota(jnp.int32, (256, 256), 0)
    col_i = lax.broadcasted_iota(jnp.int32, (256, 256), 1)
    perm = jnp.where(
        ((row_i & 31) == (col_i >> 3)) & ((row_i >> 5) == (col_i & 7)), 1.0, 0.0
    ).astype(BF)

    def relay_out(lo, hi):
        def body(it, carry):
            base = pl.multiple_of(it * 512, 512)
            out_base = pl.multiple_of(it * 64, 64)
            rhs = jnp.concatenate(
                [wraw[pl.ds(base, 256), :], wraw[pl.ds(base + 256, 256), :]], axis=1
            )
            res = dot(perm, rhs).astype(BF)
            for e in range(8):
                for s in range(2):
                    wrel[pl.ds(out_base + 32 * s, 32), 128 * e : 128 * (e + 1)] = res[
                        32 * e : 32 * (e + 1), 128 * s : 128 * (s + 1)
                    ]
            return carry

        lax.fori_loop(lo, hi, body, 0)

    ld_wqkv.wait()

    def project(block, slot):
        xf = block.astype(F32)
        return [dot(block, wqkv[i, slot]) for i in range(3)], jnp.sum(
            xf * xf, axis=-1, keepdims=True
        )

    proj, squares = project(hidden_ref[...], me_h)
    for k in (1, 7, 6, 2, 3, 5, 4):
        got_hid[k].wait_recv()
        slot = (me_h + 8 - k) % 8
        more, sq = project(hid[slot], slot)
        proj = [a + b for a, b in zip(proj, more)]
        squares = squares + sq
    rs = lax.rsqrt(squares * (1.0 / D) + norm_eps)
    q_f, k_f, v_f = [], [], []
    for h in range(2):
        part = [p[:, HD * h : HD * (h + 1)] * rs for p in proj]

        def turned(v):
            swapped = jnp.concatenate([v[:, HD // 2 :], v[:, : HD // 2]], axis=1)
            return (v * cosine + swapped * sine).astype(BF).astype(F32)

        q_f.append(turned(part[0]))
        k_f.append(turned(part[1]))
        v_f.append(part[2].astype(BF).astype(F32))
        qs[h] = q_f[h]

    pl.semaphore_wait(plane_sem, 3)
    for k in range(1, 4):
        tell(cube_sem, at(0, k, 0))

    def send_share(i, carry):
        remote(tshare.at[z, x], tshare.at[z, x], t_s, t_r, at(i // 4, 0, i % 4)).start()
        return carry

    lax.fori_loop(1, 16, send_share, 0)

    for copy in ld_k:
        copy.wait()
    owner16 = lax.broadcasted_iota(jnp.int32, (16, COLS), 0) & 7
    owner16s = lax.broadcasted_iota(jnp.int32, (16, HD), 0) & 7

    def score_group(g, carry):
        base = pl.multiple_of(g * 8, 8)
        query = qs[:, pl.ds(base, 8), :].reshape(16, HD).astype(BF)
        out = None
        for i in range(8):
            s = lax.dot_general(
                query, kbuf[g * 8 + i], (((1,), (1,)), ((), ())), preferred_element_type=F32
            )
            out = s if i == 0 else jnp.where(owner16 == i, s, out)
        sc[:, pl.ds(base, 8), :] = out.reshape(2, 8, COLS)
        return carry

    lax.fori_loop(0, 4, score_group, 0)

    position = lax.broadcasted_iota(jnp.int32, (ROWS, COLS), 1)
    self_w = []
    for h in range(2):
        valid = ((position & 1) == h) & (position < limit)
        s = jnp.where(valid, sc[h] * SCALE, -jnp.inf)
        self_score = jnp.sum(q_f[h] * k_f[h], axis=-1, keepdims=True) * SCALE
        top = jnp.maximum(jnp.max(s, axis=-1, keepdims=True), self_score)
        e = jnp.exp(s - top)
        self_e = jnp.exp(self_score - top)
        inv = 1.0 / (jnp.sum(e, axis=-1, keepdims=True) + self_e)
        sc[h] = e * inv
        self_w.append((self_e * inv).astype(BF).astype(F32))

    for copy in ld_v:
        copy.wait()

    def value_group(g, carry):
        base = pl.multiple_of(g * 8, 8)
        weights = sc[:, pl.ds(base, 8), :].reshape(16, COLS).astype(BF)
        out = None
        for i in range(8):
            s = dot(weights, vbuf[g * 8 + i])
            out = s if i == 0 else jnp.where(owner16s == i, s, out)
        att[:, pl.ds(base, 8), :] = out.reshape(2, 8, HD)
        return carry

    lax.fori_loop(0, 4, value_group, 0)
    attended = jnp.concatenate(
        [(att[h] + self_w[h] * v_f[h]).astype(BF) for h in range(2)], axis=1
    )

    for copy in ld_wout:
        copy.wait()
    got_c = {}
    for k in order:
        peer = (me_h + k) % 8
        cts[peer] = dot(attended, wout[peer]).astype(BF)
        got_c[k] = push(
            cts.at[peer], ctr.at[me_h], cs_sem.at[k - 1], cr_sem.at[k - 1], (me_r, peer)
        )
    mine = dot(attended, wout[me_h]).astype(BF).astype(F32)
    ld_win.wait()
    relay_out(0, 16)
    total = hidden_ref[...].astype(F32) + mine
    for k in (1, 7, 6, 2, 3, 5, 4):
        got_c[k].wait_recv()
        total = total + ctr[(me_h + 8 - k) % 8].astype(F32)
    resid[...] = total
    gath[z, c, y, x] = total.astype(BF)

    pl.semaphore_wait(cube_sem, 3)
    def spread(dz):
        def send_rows(i, carry):
            remote(
                gath.at[z, c, y, x], gath.at[z, c, y, x], d_s, d_r.at[(4 - dz) % 4],
                at(i // 4, i % 4, dz),
            ).start()
            return carry

        lax.fori_loop(1 if dz == 0 else 0, 16, send_rows, 0)

    spread(2)
    relay_out(16, 24)
    spread(1)
    spread(3)
    relay_out(24, 32)
    remote(
        kbuf.at[pl.ds(0, 15), pl.ds(0, ROWS)], kbuf.at[pl.ds(0, 15), pl.ds(0, ROWS)],
        t_s, t_r, other,
    ).wait_recv()

    def collect(g):
        zz = (z + g) % 4
        whole = yrecv.at[pl.ds(0, 15 if g == 0 else 16)]
        remote(whole, whole, d_s, d_r.at[g], other).wait_recv()
        return push(gath.at[zz, c], gath.at[zz, c], dd_s.at[g], dd_r.at[g], other)

    e_row = lax.broadcasted_iota(jnp.int32, (128, HD), 0)
    e_lane = lax.broadcasted_iota(jnp.int32, (128, HD), 1)

    def gate_up(group):
        m = 128 * len(group)
        scales, shares = [], []
        for i, g in enumerate(group):
            zz = (z + g) % 4
            part = None
            for j in range(8):
                block = gath[zz, j % 2, j // 2].reshape(128, 256)
                xs[128 * i : 128 * (i + 1), 256 * j : 256 * (j + 1)] = block
                f = block.astype(F32)
                f = f * f
                f = f[:, :128] + f[:, 128:]
                part = f if part is None else part + f
            mean = jnp.sum(part, axis=-1, keepdims=True) * (1.0 / D)
            scales.append(lax.rsqrt(mean + norm_eps))
            shares.append(tshare[zz].reshape(128, 128))
        scale = jnp.concatenate(scales, axis=0)
        shares = jnp.concatenate(shares, axis=0)
        low = lax.broadcasted_iota(jnp.int32, (m, HD), 1) < 64

        def body(n, carry):
            cols = pl.ds(pl.multiple_of(n * 256, 256), 256)
            got = dot(xs[:m, :], wrel[:, cols])
            pick = jnp.where(
                (e_row < 16) & ((e_row & 7) == 2 * n + (e_lane >> 6)), 1.0, 0.0
            ).astype(BF)
            share = dot(shares, pick)
            even = got[:, :128] * scale
            odd = got[:, 128:] * scale
            gate = jnp.where(low, even, pltpu.roll(odd, 64, 1))
            upward = jnp.where(low, pltpu.roll(even, 64, 1), odd)
            silu = gate / (1.0 + jnp.exp(-gate))
            units[:m, pl.ds(pl.multiple_of(n * 128, 128), 128)] = (
                share * (silu * upward)
            ).astype(BF)
            return carry

        lax.fori_loop(0, 4, body, 0)

    turns = (2, 1, 3, 0)
    got_x = {}

    def give(group):
        m = 128 * len(group)
        for dy in turns:
            val = dot(units[:m, :], wdown[((y + dy) % 4) * 2 + (1 - c)]).astype(BF)
            for i, g in enumerate(group):
                psend[g, dy] = val[128 * i : 128 * (i + 1)].reshape(4, ROWS, 256)
                got_x[g, dy] = push(
                    psend.at[g, dy], xrecv.at[g, dy], ps_s.at[g, dy], ps_r.at[g, dy], other
                )

    def keep(group):
        m = 128 * len(group)
        for dy in turns:
            val = dot(units[:m, :], wdown[((y + dy) % 4) * 2 + c])
            for i, g in enumerate(group):
                got_x[g, dy].wait_recv()
                mine = val[128 * i : 128 * (i + 1)] + xrecv[g, dy].reshape(128, 256).astype(F32)
                ssum[g, dy] = mine.astype(BF).reshape(4, ROWS, 256)

                def send_sum(dx, carry, dy=dy, g=g):
                    xx = (x + dx) % 4
                    slot = ((4 - g) % 4) * 16 + ((4 - dx) % 4) * 4 + (4 - dy) % 4
                    remote(
                        ssum.at[g, dy, xx], yrecv.at[slot], e_s, e_r.at[(4 - g) % 4],
                        at(dx, dy, g),
                    ).start()
                    return carry

                lax.fori_loop(1 if g == 0 and dy == 0 else 0, 4, send_sum, 0)

    for copy in ld_wdown:
        copy.wait()
    first = collect(2)
    spread(0)
    first.wait_recv()
    gate_up((2,))
    give((2,))
    near = [collect(1), collect(3)]
    keep((2,))
    for copy in near:
        copy.wait_recv()
    gate_up((1, 3))
    give((1, 3))
    last = collect(0)
    keep((1, 3))
    last.wait_recv()
    gate_up((0,))
    give((0,))
    keep((0,))

    result = resid[...] + ssum[0, 0, x].astype(F32)
    for g in (2, 1, 3, 0):
        first_slot = 16 * g + (1 if g == 0 else 0)
        slots = pl.ds(first_slot, 15 if g == 0 else 16)
        remote(yrecv.at[slots], yrecv.at[slots], e_s, e_r.at[g], other).wait_recv()
        for i in range(first_slot, 16 * g + 16):
            result = result + yrecv[i].astype(F32)
    out_ref[...] = result.astype(BF)
    for copy in sends:
        copy.wait_send()
    cells = yrecv.at[pl.ds(1, 63)]
    remote(cells, cells, d_s, d_r.at[0], other).wait_send()
    remote(cells, cells, e_s, e_r.at[0], other).wait_send()
    few = kbuf.at[pl.ds(0, 15), pl.ds(0, ROWS)]
    remote(few, few, t_s, t_r, other).wait_send()


def layer(hidden, lengths, expert_ids, route_weights, w_qkv, w_out, k_cache, v_cache, w_in, w_down):
    half = HD // 2
    freqs = np.tile(rope_theta ** (-np.arange(half, dtype=np.float64) / half), 2)
    sign = np.repeat([-1.0, 1.0], half)

    vm = pl.BlockSpec(memory_space=pltpu.VMEM)
    hbm = pl.BlockSpec(memory_space=pl.ANY)
    V = pltpu.VMEM
    dma = pltpu.SemaphoreType.DMA
    regular = pltpu.SemaphoreType.REGULAR
    return pl.pallas_call(
        kernel,
        out_shape=jax.ShapeDtypeStruct((ROWS, 256), BF),
        in_specs=[vm] * 6 + [hbm] * 6,
        out_specs=vm,
        scratch_shapes=[
            V((3, 8, 256, 256), BF), V((8, 256, 256), BF), V((ROWS, COLS, HD), BF),
            V((ROWS, COLS, HD), BF), V((16384, 128), BF), V((2048, 1024), BF), V((8, 512, 256), BF),
            V((8, ROWS, 256), BF), V((2, ROWS, HD), F32), V((2, ROWS, COLS), F32),
            V((2, ROWS, HD), F32), V((8, ROWS, 256), BF), V((8, ROWS, 256), BF),
            V((ROWS, 256), F32), V((4, 2, 4, 4, ROWS, 256), BF), V((4, 4, ROWS, 128), BF),
            V((256, D), BF), V((256, 512), BF),
            V((4, 4, 4, ROWS, 256), BF), V((4, 4, 4, ROWS, 256), BF), V((4, 4, 4, ROWS, 256), BF),
            V((64, ROWS, 256), BF),
            dma((26,)), dma((7,)), dma((7,)), dma((7,)), dma((7,)), dma, dma, dma, dma((4,)),
            dma((4,)), dma((4,)), dma((4, 4)), dma((4, 4)), dma, dma((4,)), regular, regular,
        ],
        compiler_params=pltpu.CompilerParams(
            collective_id=0, has_side_effects=True, vmem_limit_bytes=60 * 1024 * 1024
        ),
    )(
        jnp.asarray(freqs.astype(np.float32)[None, :]), jnp.asarray(sign.astype(np.float32)[None, :]),
        hidden, lengths[None, :], expert_ids.T, route_weights.T,
        w_qkv.reshape(3, 8, 256, 256), w_out,
        k_cache.reshape(ROWS, COLS, HD), v_cache.reshape(ROWS, COLS, HD),
        w_in.reshape(16384, 128), w_down.reshape(512, D),
    )


def solution(mesh):
    in_specs = (
        P("req", "head"),
        P("req"),
        P("req", None),
        P("req", None),
        P(None, None, "head"),
        P("head", None),
        P("req", None, "head", None),
        P("req", None, "head", None),
        P(None, "head", "req"),
        P("head", "req", None),
    )
    return jax.shard_map(
        layer, mesh=mesh, in_specs=in_specs, out_specs=P("req", "head"), check_vma=False
    )
```
